128 devices in a mesh: sec: 4 (over x), op: 32 (over z, y, core).
Axes of the slice: x: 4, y: 4, z: 4, core: 2. Of those that a mesh axis runs over, the one named last changes fastest.
Arguments:
- wavefunction: bfloat16 [4, 1024, 1024], P('sec'), may hold values from -6 to 6
- left_operator: bfloat16 [128, 4, 1024, 1024], P('op', 'sec'), may hold values from -0.011048543 to 0.35355339
- right_operator: bfloat16 [128, 1024, 1024], P('op'), may hold values from -0.125 to 1.125
- sector_size: int32 [4], replicated, may hold values from 512 to 1024
- term_shift: int32 [128], replicated, may hold values from 0 to 3, as said below
Outputs:
- sigma: float32 [4, 1024, 1024], P('sec', 'op')
- residual: float32 [4, 1024, 1024], P('sec', 'op')
The draws below stay inside these ranges and needn't reach their ends.
Inputs may be any that keep to these rules, and one draw needn't show every extreme that they name: `term_shift`: among the 4 terms of one index of op (terms g * 4 to g * 4 + 3), the shifts are distinct.
All inputs are finite; a program needn't handle non-finite values.
Results may differ from the reference program's by a relative error of at most 0.0025.
Values may be sent and summed in bfloat16 or wider, within the bound.
A program may use at most 128 MiB of HBM per device.

```python
import jax
import jax.numpy as jnp
from jax import lax

M = 1024
K = 1024
TERM_DEV = 4
TERMS = 128
SECTORS = 4


def draw_term_shift(key, part):
    groups = TERMS // TERM_DEV
    keys = jax.random.split(jax.random.fold_in(key, 17), groups)
    orders = jax.vmap(lambda single: jax.random.permutation(single, SECTORS))(keys)
    return orders[:, :TERM_DEV].reshape(-1).astype(jnp.int32)


def dense_noise(key, shape):
    noise = jnp.clip(jax.random.normal(key, shape, jnp.float32), -4.0, 4.0)
    return noise


def draw_wavefunction(key, part):
    keys = jax.random.split(jax.random.fold_in(key, 53), 3)
    shared_weight = 0.6
    own_weight = (1.0 - shared_weight * shared_weight) ** 0.5
    common = dense_noise(keys[0], (M, K))
    own = dense_noise(keys[1], (SECTORS, M, K))
    row_scale = 10.0 ** jax.random.uniform(keys[2], (SECTORS, M), jnp.float32, -0.5, 0.5)
    value = row_scale[:, :, None] * (shared_weight * common[None] + own_weight * own)
    return jnp.clip(value, -6.0, 6.0).astype(jnp.bfloat16)


def draw_left_operator(key, part):
    keys = jax.random.split(jax.random.fold_in(key, 29), 5)
    order = jax.random.permutation(keys[0], SECTORS).astype(jnp.float32)
    offsets = jax.random.uniform(keys[1], (SECTORS,), jnp.float32)
    base = 0.25 * 10.0 ** ((order + offsets) / SECTORS)
    factor = jax.random.uniform(keys[2], (TERMS, SECTORS), jnp.float32, 0.6, 1.4)
    strength = base[None, :] * factor
    indices = jnp.arange(M, dtype=jnp.int32)
    ramp = 0.25 + 0.75 * indices.astype(jnp.float32) / M
    rough = jax.random.uniform(keys[4], (TERMS, SECTORS, M), jnp.float32, 0.5, 1.0)
    diagonal_part = strength[:, :, None] * ramp[None, None, :] * rough
    identity = (indices[:, None] == indices[None, :]).astype(jnp.float32)
    noise = dense_noise(keys[3], (TERMS, SECTORS, M, M))
    block = diagonal_part[:, :, :, None] * identity[None, None] + noise * M ** (-0.5)
    return (block * TERMS ** (-0.5)).astype(jnp.bfloat16)


def draw_right_operator(key, part):
    keys = jax.random.split(jax.random.fold_in(key, 41), 1)
    indices = jnp.arange(K, dtype=jnp.int32)
    identity = (indices[:, None] == indices[None, :]).astype(jnp.float32)
    noise = dense_noise(keys[0], (TERMS, K, K))
    block = identity[None] + noise * K ** (-0.5)
    return block.astype(jnp.bfloat16)


def set_ends(drawn, key, least, top_value):
    longest = drawn.shape.index(max(drawn.shape))
    spots = []
    for shift in (0, 1):
        where = [jax.random.randint(jax.random.fold_in(key, axis), (), 0, length) for axis, length in enumerate(drawn.shape)]
        where[longest] = (where[longest] + shift) % drawn.shape[longest]
        spots.append(tuple(where))
    return drawn.at[spots[0]].set(least).at[spots[1]].set(top_value)


def setup_inputs(seed: int = 0) -> dict:
    key_list = jax.random.split(jax.random.key(seed), 6)
    return {
        "wavefunction": draw_wavefunction(jax.random.fold_in(key_list[5], 71), 0),
        "left_operator": draw_left_operator(jax.random.fold_in(key_list[5], 71), 0),
        "right_operator": draw_right_operator(jax.random.fold_in(key_list[5], 71), 0),
        "sector_size": set_ends(jax.random.randint(key_list[3], (SECTORS,), M // 2, M + 1), jax.random.fold_in(key_list[3], 1), M // 2, M).astype(jnp.int32),
        "term_shift": draw_term_shift(jax.random.fold_in(key_list[5], 71), 0),
    }


def reference(wavefunction, left_operator, right_operator, sector_size, term_shift):
    positions = jnp.arange(M, dtype=jnp.int32)
    row_mask = (positions[None, :] < sector_size[:, None]).astype(jnp.float32)
    masked = (wavefunction.astype(jnp.float32) * row_mask[:, :, None]).astype(jnp.bfloat16)
    sectors = jnp.arange(SECTORS, dtype=jnp.int32)

    def add_term(total, item):
        left_block, right_block, shift = item
        left_image = jnp.einsum("smn,snk->smk", left_block.astype(jnp.float32), masked.astype(jnp.float32)).astype(jnp.bfloat16)
        right_image = jnp.einsum("smk,kl->sml", left_image.astype(jnp.float32), right_block.astype(jnp.float32)).astype(jnp.bfloat16)
        targets = (sectors + shift) % SECTORS
        moving = (sectors[:, None] == targets[None, :]).astype(jnp.float32)
        total = total + jnp.einsum("as,smk->amk", moving, right_image.astype(jnp.float32))
        return total, None

    start = jnp.zeros((SECTORS, M, K), jnp.float32)
    gathered, unused = lax.scan(add_term, start, (left_operator, right_operator, term_shift))
    sigma = gathered * row_mask[:, :, None]
    state = masked.astype(jnp.float32)
    energy = jnp.sum(state * sigma) / jnp.sum(state * state)
    residual = sigma - energy * state
    return sigma, residual
```

```python
import jax
import jax.numpy as jnp
from jax import lax
from jax.experimental import pallas as pl
from jax.experimental.pallas import tpu as pltpu
from jax.sharding import Mesh
from jax.sharding import PartitionSpec as P

OP = ("op_0", "op_1", "op_2")
AXES = ("sec", "op_0", "op_1", "op_2")
MESH = pl.DeviceIdType.MESH
BF = jnp.bfloat16
F32 = jnp.float32
PAIRS = 8
ITEMS = 16
LAG = 4


def decode(p):
    own = lax.div(p, 6)
    far = 1 - own
    return far * lax.div(p, 3) + own * (p - 6), far * lax.rem(p, 3) + own * 3


def fold(v):
    v = jnp.sum(v.reshape(-1, 8, 256), axis=0)
    return v[:, :128] + v[:, 128:]


def kernel(
    shift, size, psi, psi_rows, left, right, sig_out, res_out,
    psib, left0, left1, right0, right1, image, rowsb,
    c_send, c_recv, sy, sz, ry, rz, ty, tz, rxy, rxz, toy, toz, uy, uz, ruy, ruz,
    acc, red, red_c, red_x, red_y, red_z,
    load_sem, send_sem, c_sem, y_sem, z_sem, xy_sem, xz_sem, uy_sem, uz_sem, red_send, red_recv,
):
    x, z, y, c = (lax.axis_index(a) for a in AXES)
    group = z * 8 + y * 2 + c
    live = size[x]

    def ring(me, d):
        return lax.rem(me + d, 4)

    leftb = (left0, left1)
    rightb = (right0, right1)
    psi_cp = pltpu.make_async_copy(psi, psib, load_sem.at[0])
    halves = (1 - c, c)
    left_cp = [
        [
            pltpu.make_async_copy(left.at[:, :, :, halves[f], b], leftb[b].at[:, f], load_sem.at[1 + 2 * b + f])
            for f in range(2)
        ]
        for b in range(2)
    ]
    right_cp = [
        pltpu.make_async_copy(right.at[:, :, pl.ds(h * 512, 512)], rightb[h], load_sem.at[5 + h]) for h in range(2)
    ]
    rows_cp = [
        pltpu.make_async_copy(
            psi_rows.at[:, :, c, b, :, pl.ds(h * 512, 512)], rowsb.at[b, h], load_sem.at[7 + 2 * b + h]
        )
        for b in range(2)
        for h in range(2)
    ]
    psi_cp.start()
    for cp in left_cp[0]:
        cp.start()
    for cp in right_cp:
        cp.start()
    for cp in left_cp[1] + rows_cp:
        cp.start()

    barrier = pltpu.get_barrier_semaphore()
    for d in range(1, 4):
        for axis, me in (("sec", x), ("op_0", z), ("op_1", y)):
            pl.semaphore_signal(barrier, inc=1, device_id={axis: ring(me, d)}, device_id_type=MESH)
    pl.semaphore_signal(barrier, inc=1, device_id={"op_2": 1 - c}, device_id_type=MESH)
    pl.semaphore_wait(barrier, 10)

    psi_cp.wait()

    @pl.loop(0, 4)
    def _(i):
        r = pl.multiple_of(512 + i * 128, 128)
        pos = lax.broadcasted_iota(jnp.int32, (128, 1024), 0) + r
        psib[pl.ds(r, 128), :] = jnp.where(pos < live, psib[pl.ds(r, 128), :].astype(F32), 0.0).astype(BF)

    def term_of(k):
        want = lax.rem(k + 1, 4)
        t = jnp.int32(0)
        for i in range(1, 4):
            t = jnp.where(shift[group * 4 + i] == want, i, t)
        return t

    def to(axis, where, src, dst, sem_s, sem_r):
        return pltpu.make_async_remote_copy(
            src_ref=src, dst_ref=dst, send_sem=sem_s, recv_sem=sem_r, device_id={axis: where}, device_id_type=MESH
        )

    def drain(ref, sem):
        pltpu.make_async_copy(ref, ref, sem).wait()

    def core_copy(n):
        return to("op_2", 1 - c, c_send.at[n], c_recv.at[n], send_sem.at[0], c_sem.at[n])

    def left_step(p, held):
        t = term_of(decode(p)[1])
        slot = lax.rem(p, 2)
        a = held[t].reshape(512, 1024)
        for q in range(4):
            cols = slice(q * 256, (q + 1) * 256)
            o = jnp.dot(a, psib[:, cols], preferred_element_type=F32).astype(BF)
            image[slot, :, :, cols] = o.reshape(2, 256, 256)

    def partner_half(p, h):
        t = term_of(decode(p)[1])
        n = p * 2 + h
        a = image[lax.rem(p, 2), 0]
        for q in range(2):
            cols = slice(q * 256, (q + 1) * 256)
            c_send[n, :, cols] = jnp.dot(a, rightb[h][t, :, cols], preferred_element_type=F32).astype(BF)
        core_copy(n).start()

    def own_half(p, h):
        b, k = decode(p)
        t = term_of(k)
        n = p * 2 + h
        core_copy(n).wait_recv()
        a = image[lax.rem(p, 2), 1]
        for q in range(2):
            cols = slice(q * 256, (q + 1) * 256)
            v = jnp.dot(a, rightb[h][t, :, cols], preferred_element_type=F32).astype(BF).astype(F32)
            v = (v + c_recv[n, :, cols].astype(F32)).astype(BF).reshape(4, 4, 16, 256)
            if q == 0:
                for i in range(4):
                    sy[n, i] = v[:, i]
            else:
                sz[n] = v
        for d in range(1, 4):
            to("op_1", ring(y, d), sy.at[n, ring(y, d)], ry.at[n, d - 1], send_sem.at[1], y_sem.at[n]).start()
            to("op_0", ring(z, d), sz.at[n, ring(z, d)], rz.at[n, d - 1], send_sem.at[2], z_sem.at[n]).start()

        @pl.when(k == 3)
        def _():
            part = jnp.zeros((8, 128), F32)
            for i in range(4):
                part += fold(sy[n, i].astype(F32) * rowsb[b, h, :, i, :, 0:256].astype(F32))
                part += fold(sz[n, i].astype(F32) * rowsb[b, h, i, :, :, 256:512].astype(F32))
            acc[0:8] += part

    def x_copies(g, k):
        who = ring(x, k + 1)
        return (
            to("sec", who, ty.at[g, k], rxy.at[g, k], send_sem.at[3], xy_sem.at[g]),
            to("sec", who, tz.at[g, k], rxz.at[g, k], send_sem.at[4], xz_sem.at[g]),
        )

    def second(n):
        b, k = decode(lax.div(n, 2))
        g = b * 2 + lax.rem(n, 2)
        drain(ry.at[n], y_sem.at[n])
        drain(rz.at[n], z_sem.at[n])
        vy = sy[n, y].astype(F32)
        vz = sz[n, z].astype(F32)
        for d in range(3):
            vy += ry[n, d].astype(F32)
            vz += rz[n, d].astype(F32)

        @pl.when(k < 3)
        def _():
            ty[g, k] = vy.astype(BF)
            tz[g, k] = vz.astype(BF)
            for cp in x_copies(g, k):
                cp.start()

        @pl.when(k == 3)
        def _():
            toy[g] = vy
            toz[g] = vz

    @pl.loop(0, PAIRS + 1)
    def _(p):
        @pl.when(p == 0)
        def _():
            acc[...] = jnp.zeros_like(acc)
            for cp in left_cp[0]:
                cp.wait()

        @pl.when(p == 3)
        def _():
            for cp in left_cp[1]:
                cp.wait()

        for b in range(2):

            @pl.when((p < PAIRS) & (decode(p)[0] == b))
            def _():
                left_step(p, leftb[b])

        @pl.when(p == 0)
        def _():
            right_cp[0].wait()

        @pl.when(p < PAIRS)
        def _():
            partner_half(p, 0)

        @pl.when(p >= 1)
        def _():
            own_half(p - 1, 1)

        @pl.when(p == 0)
        def _():
            right_cp[1].wait()

        @pl.when(p < PAIRS)
        def _():
            partner_half(p, 1)
            own_half(p, 0)

        @pl.when(p == 3)
        def _():
            for cp in rows_cp:
                cp.wait()
            for b in range(2):
                for h in range(2):
                    for i in range(4):
                        pos = (
                            lax.broadcasted_iota(jnp.int32, (4, 16, 512), 0) * 64
                            + lax.broadcasted_iota(jnp.int32, (4, 16, 512), 1)
                            + (i * 256 + c * 32 + b * 16)
                        )
                        rowsb[b, h, i] = jnp.where(pos < live, rowsb[b, h, i].astype(F32), 0.0).astype(BF)
            norm = jnp.zeros((8, 128), F32)
            for b in range(2):
                for h in range(2):
                    s = rowsb[b, h, z, y].astype(F32)
                    norm += fold(s[:, :256] * s[:, :256]) + fold(s[:, 256:] * s[:, 256:])
            acc[8:16] = norm

        for i in range(2):

            @pl.when((p * 2 + i >= LAG) & (p < PAIRS))
            def _():
                second(p * 2 + i - LAG)

    for g in range(4):
        b, h = divmod(g, 2)
        drain(rxy.at[g], xy_sem.at[g])
        drain(rxz.at[g], xz_sem.at[g])
        ay = rxy[g, 0].astype(F32) + rxy[g, 1].astype(F32) + rxy[g, 2].astype(F32)
        az = rxz[g, 0].astype(F32) + rxz[g, 1].astype(F32) + rxz[g, 2].astype(F32)
        acc[0:8] += fold(ay * rowsb[b, h, :, y, :, 0:256].astype(F32)) + fold(
            az * rowsb[b, h, z, :, :, 256:512].astype(F32)
        )

    def red_start(stage, axis, me, n, dst):
        for d in range(1, n):
            to(axis, lax.rem(me + d, n), red.at[stage], dst.at[d - 1], red_send.at[stage], red_recv.at[stage]).start()

    def red_finish(stage, n, dst):
        drain(dst, red_recv.at[stage])
        v = red[stage]
        for d in range(n - 1):
            v += dst[d]
        red[stage + 1] = v

    red[0] = acc[...]
    red_start(0, "op_2", c, 2, red_c)

    @pl.loop(ITEMS - LAG, ITEMS - 1)
    def _(n):
        second(n)

    red_finish(0, 2, red_c)
    red_start(1, "sec", x, 4, red_x)
    second(jnp.int32(ITEMS - 1))
    for g in range(4):
        vy = toy[g]
        vz = toz[g]
        for d in range(3):
            vy += rxy[g, d].astype(F32)
            vz += rxz[g, d].astype(F32)
        toy[g] = vy
        toz[g] = vz
        uy[g] = vy.astype(BF)
        uz[g] = vz.astype(BF)
        for d in range(1, 4):
            to("op_0", ring(z, d), uy.at[g, ring(z, d)], ruy.at[g, d - 1], send_sem.at[5], uy_sem.at[g]).start()
            to("op_1", ring(y, d), uz.at[g, ring(y, d)], ruz.at[g, d - 1], send_sem.at[6], uz_sem.at[g]).start()
    red_finish(1, 4, red_x)
    red_start(2, "op_1", y, 4, red_y)
    for g in range(4):
        b, h = divmod(g, 2)
        drain(ruy.at[g], uy_sem.at[g])
        drain(ruz.at[g], uz_sem.at[g])
        vy = toy[g, z]
        vz = toz[g, y]
        for d in range(3):
            vy += ruy[g, d].astype(F32)
            vz += ruz[g, d].astype(F32)
        first = z * 256 + y * 64 + c * 32 + b * 16
        keep = first + lax.broadcasted_iota(jnp.int32, (16, 256), 0) < live
        sig_out[b * 16 : b * 16 + 16, h * 512 : h * 512 + 256] = jnp.where(keep, vy, 0.0)
        sig_out[b * 16 : b * 16 + 16, h * 512 + 256 : h * 512 + 512] = jnp.where(keep, vz, 0.0)
    red_finish(2, 4, red_y)
    red_start(3, "op_0", z, 4, red_z)
    drain(red_z, red_recv.at[3])
    total = red[3] + red_z[0] + red_z[1] + red_z[2]
    energy = jnp.sum(total[0:8]) / jnp.sum(total[8:16])
    for b in range(2):
        for h in range(2):
            at = (slice(b * 16, b * 16 + 16), slice(h * 512, h * 512 + 512))
            res_out[at] = sig_out[at] - energy * rowsb[b, h, z, y].astype(F32)

    drain(c_send, send_sem.at[0])
    drain(ry, send_sem.at[1])
    drain(rz, send_sem.at[2])
    drain(ty, send_sem.at[3])
    drain(tz, send_sem.at[4])
    drain(ruy, send_sem.at[5])
    drain(ruz, send_sem.at[6])
    drain(red_c, red_send.at[0])
    drain(red_x, red_send.at[1])
    drain(red_y, red_send.at[2])
    drain(red_z, red_send.at[3])


def per_device(wavefunction, left_operator, right_operator, sector_size, term_shift):
    psi = wavefunction[0]
    hbm = pl.BlockSpec(memory_space=pl.ANY)
    smem = pl.BlockSpec(memory_space=pltpu.SMEM)
    vmem = pl.BlockSpec(memory_space=pltpu.VMEM)
    V = pltpu.VMEM
    DMA = pltpu.SemaphoreType.DMA
    out = jax.ShapeDtypeStruct((32, 1024), F32)
    sigma, residual = pl.pallas_call(
        kernel,
        out_shape=(out, out),
        in_specs=[smem, smem, hbm, hbm, hbm, hbm],
        out_specs=(vmem, vmem),
        scratch_shapes=[
            V((1024, 1024), BF),
            V((4, 2, 4, 4, 16, 1024), BF),
            V((4, 2, 4, 4, 16, 1024), BF),
            V((4, 1024, 512), BF),
            V((4, 1024, 512), BF),
            V((2, 2, 256, 1024), BF),
            V((2, 2, 4, 4, 16, 512), BF),
            V((ITEMS, 256, 512), BF),
            V((ITEMS, 256, 512), BF),
            V((ITEMS, 4, 4, 16, 256), BF),
            V((ITEMS, 4, 4, 16, 256), BF),
            V((ITEMS, 3, 4, 16, 256), BF),
            V((ITEMS, 3, 4, 16, 256), BF),
            V((4, 3, 4, 16, 256), BF),
            V((4, 3, 4, 16, 256), BF),
            V((4, 3, 4, 16, 256), BF),
            V((4, 3, 4, 16, 256), BF),
            V((4, 4, 16, 256), F32),
            V((4, 4, 16, 256), F32),
            V((4, 4, 16, 256), BF),
            V((4, 4, 16, 256), BF),
            V((4, 3, 16, 256), BF),
            V((4, 3, 16, 256), BF),
            V((16, 128), F32),
            V((4, 16, 128), F32),
            V((1, 16, 128), F32),
            V((3, 16, 128), F32),
            V((3, 16, 128), F32),
            V((3, 16, 128), F32),
            DMA((11,)),
            DMA((7,)),
            DMA((ITEMS,)),
            DMA((ITEMS,)),
            DMA((ITEMS,)),
            DMA((4,)),
            DMA((4,)),
            DMA((4,)),
            DMA((4,)),
            DMA((4,)),
            DMA((4,)),
        ],
        compiler_params=pltpu.CompilerParams(
            collective_id=0, has_side_effects=True, vmem_limit_bytes=60 * 2**20
        ),
        name="sigma_step",
    )(
        term_shift,
        sector_size,
        psi,
        psi.reshape(4, 4, 2, 2, 16, 1024),
        left_operator[:, 0].reshape(4, 4, 4, 2, 2, 16, 1024),
        right_operator,
    )
    return sigma[None], residual[None]


def solution(mesh):
    finer = Mesh(mesh.devices.reshape(mesh.shape["sec"], 4, 4, 2), AXES)
    return jax.shard_map(
        per_device,
        mesh=finer,
        in_specs=(P("sec", None, None), P(OP, "sec", None, None), P(OP, None, None), P(), P()),
        out_specs=(P("sec", OP, None), P("sec", OP, None)),
        check_vma=False,
    )
```

```python
import jax
import jax.numpy as jnp
from jax import lax
from jax.experimental import pallas as pl
from jax.experimental.pallas import tpu as pltpu
from jax.sharding import Mesh
from jax.sharding import PartitionSpec as P

OP = ("op_0", "op_1", "op_2")
AXES = ("sec", "op_0", "op_1", "op_2")
MESH = pl.DeviceIdType.MESH
BF = jnp.bfloat16
F32 = jnp.float32
PAIRS = 8
ITEMS = 16
LAG = 3


def decode(p):
    own = lax.div(p, 6)
    far = 1 - own
    return far * lax.div(p, 3) + own * (p - 6), far * lax.rem(p, 3) + own * 3


WX = 128
WY = (256, 128)
WZ = (128, 256)


def scratch():
    V = pltpu.VMEM
    DMA = pltpu.SemaphoreType.DMA
    out = {
        "psib": V((1024, 1024), BF),
        "image0": V((2, 256, 1024), BF),
        "image1": V((2, 256, 1024), BF),
        "rowsb": V((2, 2, 4, 4, 16, 512), BF),
        "c_send": V((ITEMS, 256, 512), BF),
        "c_recv": V((ITEMS, 256, 512), BF),
        "shift": pltpu.SMEM((128,), jnp.int32),
        "size": pltpu.SMEM((4,), jnp.int32),
        "sig": V((32, 1024), F32),
        "energy_row": V((1, 1024), F32),
        "unit_row": V((1, 1024), F32),
        "acc": V((16, 128), F32),
        "red": V((2, 8, 128), F32),
        "red_xy": V((15, 8, 128), F32),
        "red_zc": V((7, 8, 128), F32),
        "load_sem": DMA((13,)),
        "send_sem": DMA((20,)),
        "c_sem": DMA((ITEMS,)),
        "y_sem": DMA((ITEMS,)),
        "z_sem": DMA((ITEMS,)),
        "x_sem": DMA((4,)),
        "xy_sem": DMA((4,)),
        "xz_sem": DMA((4,)),
        "vx_sem": DMA((4,)),
        "ux_sem": DMA((4,)),
        "uy_sem": DMA((4,)),
        "uz_sem": DMA((4,)),
        "other_send": DMA((4,)),
        "other_recv": DMA((4,)),
        "red_send": DMA((2,)),
        "red_recv": DMA((2,)),
    }
    for h in range(2):
        out[f"left{h}"] = V((4, 2, 4, 4, 16, 1024), BF)
        out[f"right{h}"] = V((4, 1024, 512), BF)
        out[f"sx{h}"] = V((PAIRS, 4, 4, 16, WX), BF)
        out[f"rx{h}"] = V((2, 3, 4, 4, 16, WX), BF)
        out[f"vx{h}"] = V((2, 4, 4, 16, WX), BF)
        out[f"fx{h}"] = V((2, 4, 4, 16, WX), F32)
        out[f"rvx{h}"] = V((2, 3, 4, 16, WX), BF)
        out[f"gx{h}"] = V((2, 4, 16, WX), F32)
        out[f"ux{h}"] = V((2, 4, 16, WX), BF)
        out[f"rux{h}"] = V((2, 3, 16, WX), BF)
        for name, wide in (("y", WY[h]), ("z", WZ[h])):
            out[f"s{name}{h}"] = V((PAIRS, 4, 4, 16, wide), BF)
            out[f"r{name}{h}"] = V((PAIRS, 3, 4, 16, wide), BF)
            out[f"t{name}{h}"] = V((2, 3, 4, 16, wide), BF)
            out[f"rx{name}{h}"] = V((2, 3, 4, 16, wide), BF)
            out[f"to{name}{h}"] = V((2, 4, 16, wide), F32)
            out[f"u{name}{h}"] = V((2, 4, 16, wide), BF)
            out[f"ru{name}{h}"] = V((2, 3, 16, wide), BF)
            out[f"other{name}{h}"] = V((3, 4, 16, wide), BF)
    return out


def fold(v):
    wide = v.shape[-1]
    v = jnp.sum(v.reshape(-1, 8, wide), axis=0)
    return sum(v[:, i : i + 128] for i in range(0, wide, 128))


def kernel(shift_in, size_in, psi, psi_rows, left, right, sig_out, state_out, energy_out, unit_out, *held):
    ref = dict(zip(scratch(), held))

    def both(name):
        return ref[name + "0"], ref[name + "1"]

    psib, image0, image1, rowsb, c_send, c_recv, acc, red, red_xy, red_zc = (
        ref[name]
        for name in (
            "psib", "image0", "image1", "rowsb", "c_send", "c_recv", "acc", "red", "red_xy", "red_zc"
        )
    )
    sig, energy_row, unit_row = ref["sig"], ref["energy_row"], ref["unit_row"]
    load_sem, send_sem, c_sem, y_sem, z_sem, x_sem = (
        ref[name] for name in ("load_sem", "send_sem", "c_sem", "y_sem", "z_sem", "x_sem")
    )
    othery, otherz = both("othery"), both("otherz")
    other_send, other_recv = ref["other_send"], ref["other_recv"]
    xy_sem, xz_sem, vx_sem, ux_sem, uy_sem, uz_sem, red_send, red_recv = (
        ref[name]
        for name in ("xy_sem", "xz_sem", "vx_sem", "ux_sem", "uy_sem", "uz_sem", "red_send", "red_recv")
    )
    sx, rx, vx, fx, rvx, gx, ux, rux = (both(name) for name in ("sx", "rx", "vx", "fx", "rvx", "gx", "ux", "rux"))
    sy, ry, ty, rxy, toy, uy, ruy = (both(name) for name in ("sy", "ry", "ty", "rxy", "toy", "uy", "ruy"))
    sz, rz, tz, rxz, toz, uz, ruz = (both(name) for name in ("sz", "rz", "tz", "rxz", "toz", "uz", "ruz"))
    x, z, y, c = (lax.axis_index(a) for a in AXES)
    group = z * 8 + y * 2 + c
    shift, size = ref["shift"], ref["size"]

    def ring(me, d):
        return lax.rem(me + d, 4)

    leftb = both("left")
    rightb = both("right")
    psi_cp = pltpu.make_async_copy(psi, psib, load_sem.at[0])
    halves = (1 - c, c)
    left_cp = [
        [
            pltpu.make_async_copy(left.at[:, :, :, halves[f], b], leftb[b].at[:, f], load_sem.at[1 + 2 * b + f])
            for f in range(2)
        ]
        for b in range(2)
    ]
    right_cp = [
        pltpu.make_async_copy(right.at[:, :, pl.ds(h * 512, 512)], rightb[h], load_sem.at[5 + h]) for h in range(2)
    ]
    rows_cp = [
        pltpu.make_async_copy(
            psi_rows.at[:, :, c, b, :, pl.ds(h * 512, 512)], rowsb.at[b, h], load_sem.at[7 + 2 * b + h]
        )
        for b in range(2)
        for h in range(2)
    ]
    scalar_cp = [
        pltpu.make_async_copy(size_in, size, load_sem.at[11]),
        pltpu.make_async_copy(shift_in, shift, load_sem.at[12]),
    ]
    psi_cp.start()
    for cp in scalar_cp + left_cp[0]:
        cp.start()

    barrier = pltpu.get_barrier_semaphore()
    for d in range(1, 4):
        for e in range(4):
            pl.semaphore_signal(
                barrier, inc=1, device_id={"sec": ring(x, d), "op_1": ring(y, e)}, device_id_type=MESH
            )
        pl.semaphore_signal(barrier, inc=1, device_id={"op_1": ring(y, d)}, device_id_type=MESH)
        pl.semaphore_signal(barrier, inc=1, device_id={"op_0": ring(z, d)}, device_id_type=MESH)
        pl.semaphore_signal(barrier, inc=1, device_id={"op_0": ring(z, d), "op_2": 1 - c}, device_id_type=MESH)
    pl.semaphore_signal(barrier, inc=1, device_id={"op_2": 1 - c}, device_id_type=MESH)

    for cp in scalar_cp:
        cp.wait()
    live = size[x]
    psi_cp.wait()
    right_cp[0].start()
    for i in range(4):
        at = slice(512 + i * 128, 640 + i * 128)
        pos = lax.broadcasted_iota(jnp.int32, (128, 1024), 0) + (512 + i * 128)
        psib[at, :] = jnp.where(pos < live, psib[at, :].astype(F32), 0.0).astype(BF)
    acc[...] = jnp.zeros_like(acc)

    def term_of(k):
        want = lax.rem(k + 1, 4)
        t = jnp.int32(0)
        for i in range(1, 4):
            t = jnp.where(shift[group * 4 + i] == want, i, t)
        return t

    def send(device, src, dst, sem_s, sem_r):
        return pltpu.make_async_remote_copy(
            src_ref=src, dst_ref=dst, send_sem=sem_s, recv_sem=sem_r, device_id=device, device_id_type=MESH
        )

    def to(axis, where, src, dst, sem_s, sem_r):
        return send({axis: where}, src, dst, sem_s, sem_r)

    def drain(ref, sem):
        pltpu.make_async_copy(ref, ref, sem).wait()

    def core_copy(n):
        return to("op_2", 1 - c, c_send.at[n], c_recv.at[n], send_sem.at[0], c_sem.at[n])

    def state(b, h):
        cut = WX + WY[h]
        return (
            lambda *at: rowsb[(b, h, *at, slice(None), slice(0, WX))].astype(F32),
            lambda *at: rowsb[(b, h, *at, slice(None), slice(WX, cut))].astype(F32),
            lambda *at: rowsb[(b, h, *at, slice(None), slice(cut, 512))].astype(F32),
        )

    every = slice(None)

    def left_step(p):
        b, k = decode(p)
        t = term_of(k)
        slot = lax.rem(p, 2)
        for i in range(2):

            @pl.when(b == i)
            def _():
                a = leftb[i][t].reshape(512, 1024)
                for q in range(4):
                    cols = slice(q * 256, (q + 1) * 256)
                    o = jnp.dot(a, psib[:, cols], preferred_element_type=F32).astype(BF)
                    image0[slot, :, cols] = o[:256]
                    image1[slot, :, cols] = o[256:]

    def partner_half(p, halves):
        t = term_of(decode(p)[1])
        a = image0[lax.rem(p, 2)]
        for h in halves:
            for q in range(2):
                cols = slice(q * 256, (q + 1) * 256)
                c_send[p * 2 + h, :, cols] = jnp.dot(
                    a, rightb[h][t, :, cols], preferred_element_type=F32
                ).astype(BF)
        for h in halves:
            core_copy(p * 2 + h).start()

    def own_half(p):
        b, k = decode(p)
        t = term_of(k)
        for h in range(2):
            core_copy(p * 2 + h).wait_recv()
        a = image1[lax.rem(p, 2)]
        for h in range(2):
            for q in range(2):
                cols = slice(q * 256, (q + 1) * 256)
                v = jnp.dot(a, rightb[h][t, :, cols], preferred_element_type=F32).astype(BF).astype(F32)
                v = (v + c_recv[p * 2 + h, :, cols].astype(F32)).astype(BF).reshape(4, 4, 16, 256)
                for j in range(2):
                    w = v[..., j * 128 : (j + 1) * 128]
                    at = q * 256 + j * 128
                    if at < WX:
                        for i in range(4):
                            sx[h][p, i] = w[:, i]
                    elif at < WX + WY[h]:
                        for i in range(4):
                            sy[h][p, i, :, :, at - WX : at - WX + 128] = w[:, i]
                    else:
                        sz[h][p, :, :, :, at - WX - WY[h] : at - WX - WY[h] + 128] = w
        for h in range(2):
            n = p * 2 + h
            for d in range(1, 4):
                yd = ring(y, d)
                zd = ring(z, d)
                to("op_1", yd, sy[h].at[p, yd], ry[h].at[p, d - 1], send_sem.at[4 + h], y_sem.at[n]).start()
                to("op_0", zd, sz[h].at[p, zd], rz[h].at[p, d - 1], send_sem.at[6 + h], z_sem.at[n]).start()

        @pl.when(k < 3)
        def _():
            for h in range(2):
                to(
                    "sec", ring(x, k + 1), sx[h].at[p], rx[h].at[b, k], send_sem.at[2 + h], x_sem.at[b * 2 + h]
                ).start()

        @pl.when(k == 3)
        def _():
            for h in range(2):
                own_target(p, b, h)

    def own_target(p, b, h):
        g = b * 2 + h
        ox, oy, oz = state(b, h)
        drain(rx[h].at[b], x_sem.at[g])
        part = jnp.zeros((8, 128), F32)
        for i in range(4):
            w = sx[h][p, i].astype(F32)
            for j in range(3):
                w += rx[h][b, j, i].astype(F32)
            fx[h][b, i] = w
            vx[h][b, i] = w.astype(BF)
            part += fold(w * ox(every, i))
        for d in range(1, 4):
            yd = ring(y, d)
            to("op_1", yd, vx[h].at[b, yd], rvx[h].at[b, d - 1], send_sem.at[8 + h], vx_sem.at[g]).start()
        for i in range(4):
            part += fold(sy[h][p, i].astype(F32) * oy(every, i))
            part += fold(sz[h][p, i].astype(F32) * oz(i, every))
        acc[0:8] += part

    def second(p):
        b, k = decode(p)
        for h in range(2):
            n = p * 2 + h
            g = b * 2 + h
            drain(ry[h].at[p], y_sem.at[n])
            drain(rz[h].at[p], z_sem.at[n])
            vy = sy[h][p, y].astype(F32)
            vz = sz[h][p, z].astype(F32)
            for d in range(3):
                vy += ry[h][p, d].astype(F32)
                vz += rz[h][p, d].astype(F32)

            toy[h][b] = vy
            toz[h][b] = vz

            @pl.when(k < 3)
            def _():
                ty[h][b, k] = vy.astype(BF)
                tz[h][b, k] = vz.astype(BF)
                who = ring(x, k + 1)
                to("sec", who, ty[h].at[b, k], rxy[h].at[b, k], send_sem.at[10 + h], xy_sem.at[g]).start()
                to("sec", who, tz[h].at[b, k], rxz[h].at[b, k], send_sem.at[12 + h], xz_sem.at[g]).start()

    def cross_share(p):
        b, k = decode(p)
        there = size[ring(x, k + 1)]

        def row(outer, inner):
            return (
                lax.broadcasted_iota(jnp.int32, (4, 16, 128), 0) * outer
                + lax.broadcasted_iota(jnp.int32, (4, 16, 128), 1)
                + (inner + c * 32 + b * 16)
            )

        live_y = row(256, y * 64) < there
        live_z = row(64, z * 256) < there
        part = jnp.zeros((8, 128), F32)
        for h in range(2):
            for i in range(0, WY[h], 128):
                w = othery[h][k, :, :, i : i + 128].astype(F32)
                part += fold(ty[h][b, k, :, :, i : i + 128].astype(F32) * jnp.where(live_y, w, 0.0))
            for i in range(0, WZ[h], 128):
                w = otherz[h][k, :, :, i : i + 128].astype(F32)
                part += fold(tz[h][b, k, :, :, i : i + 128].astype(F32) * jnp.where(live_z, w, 0.0))
        acc[0:8] += part

    def mask_rows():
        for cp in rows_cp:
            cp.wait()
        for b in range(2):
            for h in range(2):
                for i in range(4):
                    pos = (
                        lax.broadcasted_iota(jnp.int32, (4, 16, 512), 0) * 64
                        + lax.broadcasted_iota(jnp.int32, (4, 16, 512), 1)
                        + (i * 256 + c * 32 + b * 16)
                    )
                    rowsb[b, h, i] = jnp.where(pos < live, rowsb[b, h, i].astype(F32), 0.0).astype(BF)
        norm = jnp.zeros((8, 128), F32)
        for b in range(2):
            for h in range(2):
                s = rowsb[b, h, z, y].astype(F32)
                norm += fold(s[:, :256] * s[:, :256]) + fold(s[:, 256:] * s[:, 256:])
        acc[8:16] = norm

    for cp in left_cp[0]:
        cp.wait()
    for cp in right_cp[1:] + left_cp[1] + rows_cp:
        cp.start()
    left_step(jnp.int32(0))
    pl.semaphore_wait(barrier, 22)
    for k in range(3):
        who = ring(x, 3 - k)
        for h in range(2):
            cols_y = pl.ds(h * 512 + WX, WY[h])
            cols_z = pl.ds(h * 512 + WX + WY[h], WZ[h])
            to("sec", who, psi_rows.at[:, y, c, 1, :, cols_y], othery[h].at[k], other_send.at[h], other_recv.at[h]).start()
            to("sec", who, psi_rows.at[z, :, c, 1, :, cols_z], otherz[h].at[k], other_send.at[2 + h], other_recv.at[2 + h]).start()
    right_cp[0].wait()
    partner_half(jnp.int32(0), (0,))
    left_step(jnp.int32(1))
    right_cp[1].wait()
    partner_half(jnp.int32(0), (1,))
    mask_rows()

    @pl.loop(1, PAIRS)
    def _(p):
        @pl.when(p == 2)
        def _():
            for cp in left_cp[1]:
                cp.wait()

        partner_half(p, (0, 1))
        own_half(p - 1)

        @pl.when(p < PAIRS - 1)
        def _():
            left_step(p + 1)

        @pl.when(p >= LAG)
        def _():
            second(p - LAG)

    for h in range(2):
        _, oy, oz = state(0, h)
        drain(rxy[h].at[0], xy_sem.at[h])
        drain(rxz[h].at[0], xz_sem.at[h])
        ay = rxy[h][0, 0].astype(F32) + rxy[h][0, 1].astype(F32) + rxy[h][0, 2].astype(F32)
        az = rxz[h][0, 0].astype(F32) + rxz[h][0, 1].astype(F32) + rxz[h][0, 2].astype(F32)
        acc[0:8] += fold(ay * oy(every, y)) + fold(az * oz(z, every))
        drain(othery[h], other_recv.at[h])
        drain(otherz[h], other_recv.at[2 + h])
    cross_share(jnp.int32(3))
    cross_share(jnp.int32(4))
    own_half(jnp.int32(PAIRS - 1))
    second(jnp.int32(5))
    cross_share(jnp.int32(5))
    groups = [(b, h) for b in range(2) for h in range(2)]

    def reduce_start(stage, dst, devices):
        for i, device in enumerate(devices):
            send(device, red.at[stage], dst.at[i], red_send.at[stage], red_recv.at[stage]).start()

    def reduce_finish(stage, dst, count):
        drain(dst, red_recv.at[stage])
        v = red[stage]
        for i in range(count):
            v += dst[i]
        return v

    unit_row[...] = jnp.ones_like(unit_row)
    state_cp = [
        pltpu.make_async_copy(
            rowsb.at[b, h, z, y],
            state_out.at[pl.ds(b * 16, 16), pl.ds(h * 512, 512)],
            load_sem.at[2 + b * 2 + h],
        )
        for b, h in groups
    ] + [pltpu.make_async_copy(unit_row, unit_out, load_sem.at[6])]
    for cp in state_cp:
        cp.start()

    red[0] = jnp.concatenate([acc[0:4] + acc[4:8], acc[8:12] + acc[12:16]], axis=0)
    plane = [{"sec": ring(x, i // 4), "op_1": ring(y, i % 4)} for i in range(1, 16)]
    reduce_start(0, red_xy, plane)

    for b in range(2):
        second(jnp.int32(PAIRS - 2 + b))
        for h in range(2):
            g = b * 2 + h
            if b == 1:
                drain(rxy[h].at[b], xy_sem.at[g])
                drain(rxz[h].at[b], xz_sem.at[g])
            vy = toy[h][b]
            vz = toz[h][b]
            for d in range(3):
                vy += rxy[h][b, d].astype(F32)
                vz += rxz[h][b, d].astype(F32)
            toy[h][b] = vy
            toz[h][b] = vz
            uy[h][b] = vy.astype(BF)
            uz[h][b] = vz.astype(BF)
            for d in range(1, 4):
                zd = ring(z, d)
                yd = ring(y, d)
                to("op_0", zd, uy[h].at[b, zd], ruy[h].at[b, d - 1], send_sem.at[14 + h], uy_sem.at[g]).start()
                to("op_1", yd, uz[h].at[b, yd], ruz[h].at[b, d - 1], send_sem.at[16 + h], uz_sem.at[g]).start()
            drain(rvx[h].at[b], vx_sem.at[g])
            v = fx[h][b, y]
            for d in range(3):
                v += rvx[h][b, d].astype(F32)
            gx[h][b] = v
            ux[h][b] = v.astype(BF)
            for d in range(1, 4):
                zd = ring(z, d)
                to("op_0", zd, ux[h].at[b, zd], rux[h].at[b, d - 1], send_sem.at[18 + h], ux_sem.at[g]).start()
    red[1] = reduce_finish(0, red_xy, 15)
    stack = [{"op_0": ring(z, i // 2), "op_2": lax.rem(c + i % 2, 2)} for i in range(1, 8)]
    reduce_start(1, red_zc, stack)
    for b, h in groups:
        g = b * 2 + h
        drain(ruy[h].at[b], uy_sem.at[g])
        drain(ruz[h].at[b], uz_sem.at[g])
        drain(rux[h].at[b], ux_sem.at[g])
        v = gx[h][b, z]
        vy = toy[h][b, z]
        vz = toz[h][b, y]
        for d in range(3):
            v += rux[h][b, d].astype(F32)
            vy += ruy[h][b, d].astype(F32)
            vz += ruz[h][b, d].astype(F32)
        first = z * 256 + y * 64 + c * 32 + b * 16
        rows = slice(b * 16, b * 16 + 16)
        at = h * 512
        cut = at + WX + WY[h]
        keep = (first + lax.broadcasted_iota(jnp.int32, (16, 512), 0)) < live
        sig[rows, at : at + WX] = jnp.where(keep[:, :WX], v, 0.0)
        sig[rows, at + WX : cut] = jnp.where(keep[:, WX : WX + WY[h]], vy, 0.0)
        sig[rows, cut : at + 512] = jnp.where(keep[:, WX + WY[h] :], vz, 0.0)
    sig_cp = pltpu.make_async_copy(sig, sig_out, load_sem.at[0])
    sig_cp.start()
    total = reduce_finish(1, red_zc, 7)
    energy = jnp.sum(total[0:4]) / jnp.sum(total[4:8])
    energy_row[...] = jnp.full((1, 1024), energy, F32)
    energy_cp = pltpu.make_async_copy(energy_row, energy_out, load_sem.at[1])
    energy_cp.start()

    drain(c_send, send_sem.at[0])
    for h in range(2):
        drain(othery[h], other_send.at[h])
        drain(otherz[h], other_send.at[2 + h])
        for i, buf in enumerate((rx, ry, rz, rvx, rxy, rxz, ruy, ruz, rux)):
            drain(buf[h], send_sem.at[2 + 2 * i + h])
    drain(red_xy, red_send.at[0])
    drain(red_zc, red_send.at[1])
    for cp in state_cp + [sig_cp, energy_cp]:
        cp.wait()


def per_device(wavefunction, left_operator, right_operator, sector_size, term_shift):
    psi = wavefunction[0]
    hbm = pl.BlockSpec(memory_space=pl.ANY)
    out = jax.ShapeDtypeStruct((32, 1024), F32)
    row = jax.ShapeDtypeStruct((1, 1024), F32)
    sigma, state, energy, unit = pl.pallas_call(
        kernel,
        out_shape=(out, jax.ShapeDtypeStruct((32, 1024), BF), row, row),
        in_specs=[hbm] * 6,
        out_specs=(hbm, hbm, hbm, hbm),
        scratch_shapes=list(scratch().values()),
        compiler_params=pltpu.CompilerParams(
            collective_id=0, has_side_effects=True, vmem_limit_bytes=60 * 2**20
        ),
        name="sigma_step",
    )(
        term_shift,
        sector_size,
        psi,
        psi.reshape(4, 4, 2, 2, 16, 1024),
        left_operator[:, 0].reshape(4, 4, 4, 2, 2, 16, 1024),
        right_operator,
    )
    sigma = sigma * unit
    return sigma[None], (sigma - energy * state.astype(F32))[None]


def solution(mesh):
    finer = Mesh(mesh.devices.reshape(mesh.shape["sec"], 4, 4, 2), AXES)
    return jax.shard_map(
        per_device,
        mesh=finer,
        in_specs=(P("sec", None, None), P(OP, "sec", None, None), P(OP, None, None), P(), P()),
        out_specs=(P("sec", OP, None), P("sec", OP, None)),
        check_vma=False,
    )
```

```python
import jax
import jax.numpy as jnp
from jax import lax
from jax.experimental import pallas as pl
from jax.experimental.pallas import tpu as pltpu
from jax.sharding import Mesh
from jax.sharding import PartitionSpec as P

OP = ("op_0", "op_1", "op_2")
AXES = ("sec", "op_0", "op_1", "op_2")
MESH = pl.DeviceIdType.MESH
BF = jnp.bfloat16
F32 = jnp.float32
PAIRS = 8
ITEMS = 16
LAG = 3


def decode(p):
    return (p // 3, p % 3) if p < 6 else (p - 6, 3)


WX = (128, 0)
WY = ((256, 128), (256, 256))
WZ = ((128, 256), (256, 256))


def scratch():
    V = pltpu.VMEM
    DMA = pltpu.SemaphoreType.DMA
    out = {
        "psib": V((1024, 1024), BF),
        "image0": V((2, 256, 1024), BF),
        "image1": V((2, 256, 1024), BF),
        "rowsb": V((2, 2, 4, 4, 16, 512), BF),
        "c_send": V((ITEMS, 256, 512), BF),
        "c_recv": V((ITEMS, 256, 512), BF),
        "shift": pltpu.SMEM((128,), jnp.int32),
        "size": pltpu.SMEM((4,), jnp.int32),
        "sig": V((32, 1024), F32),
        "energy_row": V((1, 1024), F32),
        "unit_row": V((1, 1024), F32),
        "acc": V((16, 128), F32),
        "red": V((2, 8, 128), F32),
        "red_xy": V((15, 8, 128), F32),
        "red_zc": V((7, 8, 128), F32),
        "load_sem": DMA((13,)),
        "send_sem": DMA((32,)),
        "c_sem": DMA((ITEMS,)),
        "y_sem": DMA((ITEMS,)),
        "z_sem": DMA((ITEMS,)),
        "x_sem": DMA((2,)),
        "xy_sem": DMA((4,)),
        "xz_sem": DMA((4,)),
        "vx_sem": DMA((2,)),
        "ux_sem": DMA((2,)),
        "uy_sem": DMA((4,)),
        "uz_sem": DMA((4,)),
        "other_send": DMA((4,)),
        "other_recv": DMA((4,)),
        "red_send": DMA((2,)),
        "red_recv": DMA((2,)),
    }
    for h in range(2):
        out[f"left{h}"] = V((4, 2, 4, 4, 16, 1024), BF)
        out[f"right{h}"] = V((4, 1024, 512), BF)
        out[f"sx{h}"] = V((4, 4, 4, 16, WX[0]), BF)
        out[f"rx{h}"] = V((3, 4, 4, 16, WX[0]), BF)
        out[f"vx{h}"] = V((4, 4, 16, WX[0]), BF)
        out[f"fx{h}"] = V((4, 4, 16, WX[0]), F32)
        out[f"rvx{h}"] = V((3, 4, 16, WX[0]), BF)
        out[f"gx{h}"] = V((4, 16, WX[0]), F32)
        out[f"ux{h}"] = V((4, 16, WX[0]), BF)
        out[f"rux{h}"] = V((3, 16, WX[0]), BF)
        for name, widths in (("y", WY), ("z", WZ)):
            out[f"other{name}{h}"] = V((3, 4, 16, widths[1][h]), BF)
            for b in range(2):
                wide = widths[b][h]
                out[f"s{name}{b}{h}"] = V((4, 4, 4, 16, wide), BF)
                out[f"r{name}{b}{h}"] = V((4, 3, 4, 16, wide), BF)
                out[f"t{name}{b}{h}"] = V((3, 4, 16, wide), BF)
                out[f"rx{name}{b}{h}"] = V((3, 4, 16, wide), BF)
                out[f"to{name}{b}{h}"] = V((4, 16, wide), F32)
                out[f"u{name}{b}{h}"] = V((4, 16, wide), BF)
                out[f"ru{name}{b}{h}"] = V((3, 16, wide), BF)
    return out


def fold(v):
    wide = v.shape[-1]
    v = jnp.sum(v.reshape(-1, 8, wide), axis=0)
    return sum(v[:, i : i + 128] for i in range(0, wide, 128))


def kernel(shift_in, size_in, psi, psi_rows, left, right, sig_out, state_out, energy_out, unit_out, *held):
    ref = dict(zip(scratch(), held))

    def both(name):
        return ref[name + "0"], ref[name + "1"]

    def four(name):
        return both(name + "0"), both(name + "1")

    psib, image0, image1, rowsb, c_send, c_recv, acc, red, red_xy, red_zc = (
        ref[name]
        for name in (
            "psib", "image0", "image1", "rowsb", "c_send", "c_recv", "acc", "red", "red_xy", "red_zc"
        )
    )
    sig, energy_row, unit_row = ref["sig"], ref["energy_row"], ref["unit_row"]
    load_sem, send_sem, c_sem, y_sem, z_sem, x_sem = (
        ref[name] for name in ("load_sem", "send_sem", "c_sem", "y_sem", "z_sem", "x_sem")
    )
    othery, otherz = both("othery"), both("otherz")
    other_send, other_recv = ref["other_send"], ref["other_recv"]
    xy_sem, xz_sem, vx_sem, ux_sem, uy_sem, uz_sem, red_send, red_recv = (
        ref[name]
        for name in ("xy_sem", "xz_sem", "vx_sem", "ux_sem", "uy_sem", "uz_sem", "red_send", "red_recv")
    )
    sx, rx, vx, fx, rvx, gx, ux, rux = (both(name) for name in ("sx", "rx", "vx", "fx", "rvx", "gx", "ux", "rux"))
    sy, ry, ty, rxy, toy, uy, ruy = (four(name) for name in ("sy", "ry", "ty", "rxy", "toy", "uy", "ruy"))
    sz, rz, tz, rxz, toz, uz, ruz = (four(name) for name in ("sz", "rz", "tz", "rxz", "toz", "uz", "ruz"))
    x, z, y, c = (lax.axis_index(a) for a in AXES)
    group = z * 8 + y * 2 + c
    shift, size = ref["shift"], ref["size"]

    def ring(me, d):
        return lax.rem(me + d, 4)

    leftb = both("left")
    rightb = both("right")
    psi_cp = pltpu.make_async_copy(psi, psib, load_sem.at[0])
    halves = (1 - c, c)
    left_cp = [
        [
            pltpu.make_async_copy(left.at[:, :, :, halves[f], b], leftb[b].at[:, f], load_sem.at[1 + 2 * b + f])
            for f in range(2)
        ]
        for b in range(2)
    ]
    right_cp = [
        pltpu.make_async_copy(right.at[:, :, pl.ds(h * 512, 512)], rightb[h], load_sem.at[5 + h]) for h in range(2)
    ]
    rows_cp = [
        pltpu.make_async_copy(
            psi_rows.at[:, :, c, b, :, pl.ds(h * 512, 512)], rowsb.at[b, h], load_sem.at[7 + 2 * b + h]
        )
        for b in range(2)
        for h in range(2)
    ]
    scalar_cp = [
        pltpu.make_async_copy(size_in, size, load_sem.at[11]),
        pltpu.make_async_copy(shift_in, shift, load_sem.at[12]),
    ]
    psi_cp.start()
    for cp in scalar_cp + left_cp[0]:
        cp.start()

    barrier = pltpu.get_barrier_semaphore()
    for d in range(1, 4):
        for e in range(4):
            pl.semaphore_signal(
                barrier, inc=1, device_id={"sec": ring(x, d), "op_1": ring(y, e)}, device_id_type=MESH
            )
        pl.semaphore_signal(barrier, inc=1, device_id={"op_1": ring(y, d)}, device_id_type=MESH)
        pl.semaphore_signal(barrier, inc=1, device_id={"op_0": ring(z, d)}, device_id_type=MESH)
        pl.semaphore_signal(barrier, inc=1, device_id={"op_0": ring(z, d), "op_2": 1 - c}, device_id_type=MESH)
    pl.semaphore_signal(barrier, inc=1, device_id={"op_2": 1 - c}, device_id_type=MESH)

    for cp in scalar_cp:
        cp.wait()
    live = size[x]
    psi_cp.wait()
    right_cp[0].start()
    for i in range(4):
        at = slice(512 + i * 128, 640 + i * 128)
        pos = lax.broadcasted_iota(jnp.int32, (128, 1024), 0) + (512 + i * 128)
        psib[at, :] = jnp.where(pos < live, psib[at, :].astype(F32), 0.0).astype(BF)
    acc[...] = jnp.zeros_like(acc)

    def term_of(k):
        want = (k + 1) % 4
        t = 0
        for i in range(1, 4):
            t = jnp.where(shift[group * 4 + i] == want, i, t)
        return t

    def send(device, src, dst, sem_s, sem_r):
        return pltpu.make_async_remote_copy(
            src_ref=src, dst_ref=dst, send_sem=sem_s, recv_sem=sem_r, device_id=device, device_id_type=MESH
        )

    def to(axis, where, src, dst, sem_s, sem_r):
        return send({axis: where}, src, dst, sem_s, sem_r)

    def drain(ref, sem):
        pltpu.make_async_copy(ref, ref, sem).wait()

    def core_copy(n):
        return to("op_2", 1 - c, c_send.at[n], c_recv.at[n], send_sem.at[0], c_sem.at[n])

    def state(b, h):
        wx = WX[b]
        cut = wx + WY[b][h]
        return (
            lambda *at: rowsb[(b, h, *at, slice(None), slice(0, wx))].astype(F32),
            lambda *at: rowsb[(b, h, *at, slice(None), slice(wx, cut))].astype(F32),
            lambda *at: rowsb[(b, h, *at, slice(None), slice(cut, 512))].astype(F32),
        )

    every = slice(None)

    def left_step(p):
        b, k = decode(p)
        t = term_of(k)
        slot = p % 2
        a = leftb[b][t].reshape(512, 1024)
        for q in range(4):
            cols = slice(q * 256, (q + 1) * 256)
            o = jnp.dot(a, psib[:, cols], preferred_element_type=F32).astype(BF)
            image0[slot, :, cols] = o[:256]
            image1[slot, :, cols] = o[256:]

    def partner_half(p, halves):
        t = term_of(decode(p)[1])
        a = image0[p % 2]
        for h in halves:
            for q in range(2):
                cols = slice(q * 256, (q + 1) * 256)
                c_send[p * 2 + h, :, cols] = jnp.dot(
                    a, rightb[h][t, :, cols], preferred_element_type=F32
                ).astype(BF)
        for h in halves:
            core_copy(p * 2 + h).start()

    def own_half(p):
        b, k = decode(p)
        t = term_of(k)
        for h in range(2):
            core_copy(p * 2 + h).wait_recv()
        a = image1[p % 2]
        for h in range(2):
            for q in range(2):
                cols = slice(q * 256, (q + 1) * 256)
                v = jnp.dot(a, rightb[h][t, :, cols], preferred_element_type=F32).astype(BF).astype(F32)
                v = (v + c_recv[p * 2 + h, :, cols].astype(F32)).astype(BF).reshape(4, 4, 16, 256)
                for j in range(2):
                    w = v[..., j * 128 : (j + 1) * 128]
                    at = q * 256 + j * 128
                    wx = WX[b]
                    cut = wx + WY[b][h]
                    if at < wx:
                        for i in range(4):
                            sx[h][k, i] = w[:, i]
                    elif at < cut:
                        for i in range(4):
                            sy[b][h][k, i, :, :, at - wx : at - wx + 128] = w[:, i]
                    else:
                        sz[b][h][k, :, :, :, at - cut : at - cut + 128] = w
        for h in range(2):
            n = p * 2 + h
            for d in range(1, 4):
                yd = ring(y, d)
                zd = ring(z, d)
                to("op_1", yd, sy[b][h].at[k, yd], ry[b][h].at[k, d - 1], send_sem.at[4 + 2 * b + h], y_sem.at[n]).start()
                to("op_0", zd, sz[b][h].at[k, zd], rz[b][h].at[k, d - 1], send_sem.at[8 + 2 * b + h], z_sem.at[n]).start()

        if k < 3 and WX[b]:
            for h in range(2):
                to("sec", ring(x, k + 1), sx[h].at[k], rx[h].at[k], send_sem.at[2 + h], x_sem.at[h]).start()

    def own_target(b, h):
        ox, oy, oz = state(b, h)
        part = jnp.zeros((8, 128), F32)
        if WX[b]:
            drain(rx[h], x_sem.at[h])
            for i in range(4):
                w = sx[h][3, i].astype(F32)
                for j in range(3):
                    w += rx[h][j, i].astype(F32)
                fx[h][i] = w
                vx[h][i] = w.astype(BF)
                part += fold(w * ox(every, i))
            for d in range(1, 4):
                yd = ring(y, d)
                to("op_1", yd, vx[h].at[yd], rvx[h].at[d - 1], send_sem.at[12 + h], vx_sem.at[h]).start()
        for i in range(4):
            part += fold(sy[b][h][3, i].astype(F32) * oy(every, i))
            part += fold(sz[b][h][3, i].astype(F32) * oz(i, every))
        acc[0:8] += part

    def second(p):
        b, k = decode(p)
        for h in range(2):
            n = p * 2 + h
            g = b * 2 + h
            drain(ry[b][h].at[k], y_sem.at[n])
            drain(rz[b][h].at[k], z_sem.at[n])
            vy = sy[b][h][k, y].astype(F32)
            vz = sz[b][h][k, z].astype(F32)
            for d in range(3):
                vy += ry[b][h][k, d].astype(F32)
                vz += rz[b][h][k, d].astype(F32)
            if k < 3:
                ty[b][h][k] = vy.astype(BF)
                tz[b][h][k] = vz.astype(BF)
                who = ring(x, k + 1)
                to("sec", who, ty[b][h].at[k], rxy[b][h].at[k], send_sem.at[14 + g], xy_sem.at[g]).start()
                to("sec", who, tz[b][h].at[k], rxz[b][h].at[k], send_sem.at[18 + g], xz_sem.at[g]).start()
            else:
                toy[b][h][...] = vy
                toz[b][h][...] = vz

    def cross_share(p):
        b, k = decode(p)
        there = size[ring(x, k + 1)]

        def row(outer, inner):
            return (
                lax.broadcasted_iota(jnp.int32, (4, 16, 128), 0) * outer
                + lax.broadcasted_iota(jnp.int32, (4, 16, 128), 1)
                + (inner + c * 32 + b * 16)
            )

        live_y = row(256, y * 64) < there
        live_z = row(64, z * 256) < there
        part = jnp.zeros((8, 128), F32)
        for h in range(2):
            for i in range(0, WY[1][h], 128):
                w = othery[h][k, :, :, i : i + 128].astype(F32)
                part += fold(ty[b][h][k, :, :, i : i + 128].astype(F32) * jnp.where(live_y, w, 0.0))
            for i in range(0, WZ[1][h], 128):
                w = otherz[h][k, :, :, i : i + 128].astype(F32)
                part += fold(tz[b][h][k, :, :, i : i + 128].astype(F32) * jnp.where(live_z, w, 0.0))
        acc[0:8] += part

    def mask_rows():
        for cp in rows_cp:
            cp.wait()
        for b in range(2):
            for h in range(2):
                for i in range(4):
                    pos = (
                        lax.broadcasted_iota(jnp.int32, (4, 16, 512), 0) * 64
                        + lax.broadcasted_iota(jnp.int32, (4, 16, 512), 1)
                        + (i * 256 + c * 32 + b * 16)
                    )
                    rowsb[b, h, i] = jnp.where(pos < live, rowsb[b, h, i].astype(F32), 0.0).astype(BF)
        norm = jnp.zeros((8, 128), F32)
        for b in range(2):
            for h in range(2):
                s = rowsb[b, h, z, y].astype(F32)
                norm += fold(s[:, :256] * s[:, :256]) + fold(s[:, 256:] * s[:, 256:])
        acc[8:16] = norm

    for cp in left_cp[0]:
        cp.wait()
    for cp in right_cp[1:] + left_cp[1] + rows_cp:
        cp.start()
    left_step(0)
    pl.semaphore_wait(barrier, 22)
    for k in range(3):
        who = ring(x, 3 - k)
        for h in range(2):
            cols_y = pl.ds(h * 512 + WX[1], WY[1][h])
            cols_z = pl.ds(h * 512 + WX[1] + WY[1][h], WZ[1][h])
            to("sec", who, psi_rows.at[:, y, c, 1, :, cols_y], othery[h].at[k], other_send.at[h], other_recv.at[h]).start()
            to("sec", who, psi_rows.at[z, :, c, 1, :, cols_z], otherz[h].at[k], other_send.at[2 + h], other_recv.at[2 + h]).start()
    right_cp[0].wait()
    partner_half(0, (0,))
    left_step(1)
    right_cp[1].wait()
    partner_half(0, (1,))
    mask_rows()

    for p in range(1, PAIRS):
        if p == 2:
            for cp in left_cp[1]:
                cp.wait()
        partner_half(p, (0, 1))
        own_half(p - 1)
        if p < PAIRS - 1:
            left_step(p + 1)
        else:
            for h in range(2):
                own_target(0, h)
        if p >= LAG:
            second(p - LAG)
    own_half(PAIRS - 1)

    for h in range(2):
        _, oy, oz = state(0, h)
        drain(rxy[0][h], xy_sem.at[h])
        drain(rxz[0][h], xz_sem.at[h])
        ay = rxy[0][h][0].astype(F32) + rxy[0][h][1].astype(F32) + rxy[0][h][2].astype(F32)
        az = rxz[0][h][0].astype(F32) + rxz[0][h][1].astype(F32) + rxz[0][h][2].astype(F32)
        acc[0:8] += fold(ay * oy(every, y)) + fold(az * oz(z, every))
        drain(othery[h], other_recv.at[h])
        drain(otherz[h], other_recv.at[2 + h])
    cross_share(3)
    cross_share(4)
    for h in range(2):
        own_target(1, h)
    second(5)
    cross_share(5)
    groups = [(b, h) for b in range(2) for h in range(2)]

    def reduce_start(stage, dst, devices):
        for i, device in enumerate(devices):
            send(device, red.at[stage], dst.at[i], red_send.at[stage], red_recv.at[stage]).start()

    def reduce_finish(stage, dst, count):
        drain(dst, red_recv.at[stage])
        v = red[stage]
        for i in range(count):
            v += dst[i]
        return v

    unit_row[...] = jnp.ones_like(unit_row)
    state_cp = [
        pltpu.make_async_copy(
            rowsb.at[b, h, z, y],
            state_out.at[pl.ds(b * 16, 16), pl.ds(h * 512, 512)],
            load_sem.at[2 + b * 2 + h],
        )
        for b, h in groups
    ] + [pltpu.make_async_copy(unit_row, unit_out, load_sem.at[6])]
    for cp in state_cp:
        cp.start()

    red[0] = jnp.concatenate([acc[0:4] + acc[4:8], acc[8:12] + acc[12:16]], axis=0)
    plane = [{"sec": ring(x, i // 4), "op_1": ring(y, i % 4)} for i in range(1, 16)]
    reduce_start(0, red_xy, plane)

    for b in range(2):
        second(PAIRS - 2 + b)
        for h in range(2):
            g = b * 2 + h
            if b == 1:
                drain(rxy[b][h], xy_sem.at[g])
                drain(rxz[b][h], xz_sem.at[g])
            vy = toy[b][h][...]
            vz = toz[b][h][...]
            for d in range(3):
                vy += rxy[b][h][d].astype(F32)
                vz += rxz[b][h][d].astype(F32)
            toy[b][h][...] = vy
            toz[b][h][...] = vz
            uy[b][h][...] = vy.astype(BF)
            uz[b][h][...] = vz.astype(BF)
            for d in range(1, 4):
                zd = ring(z, d)
                yd = ring(y, d)
                to("op_0", zd, uy[b][h].at[zd], ruy[b][h].at[d - 1], send_sem.at[22 + g], uy_sem.at[g]).start()
                to("op_1", yd, uz[b][h].at[yd], ruz[b][h].at[d - 1], send_sem.at[26 + g], uz_sem.at[g]).start()
            if WX[b]:
                drain(rvx[h], vx_sem.at[h])
                v = fx[h][y]
                for d in range(3):
                    v += rvx[h][d].astype(F32)
                gx[h][...] = v
                ux[h][...] = v.astype(BF)
                for d in range(1, 4):
                    zd = ring(z, d)
                    to("op_0", zd, ux[h].at[zd], rux[h].at[d - 1], send_sem.at[30 + h], ux_sem.at[h]).start()
    red[1] = reduce_finish(0, red_xy, 15)
    stack = [{"op_0": ring(z, i // 2), "op_2": lax.rem(c + i % 2, 2)} for i in range(1, 8)]
    reduce_start(1, red_zc, stack)
    for b, h in groups:
        g = b * 2 + h
        drain(ruy[b][h], uy_sem.at[g])
        drain(ruz[b][h], uz_sem.at[g])
        vy = toy[b][h][z]
        vz = toz[b][h][y]
        for d in range(3):
            vy += ruy[b][h][d].astype(F32)
            vz += ruz[b][h][d].astype(F32)
        parts = [vy, vz]
        if WX[b]:
            drain(rux[h], ux_sem.at[h])
            v = gx[h][z]
            for d in range(3):
                v += rux[h][d].astype(F32)
            parts = [v] + parts
        first = z * 256 + y * 64 + c * 32 + b * 16
        rows = slice(b * 16, b * 16 + 16)
        at = h * 512
        for v in parts:
            wide = v.shape[-1]
            keep = (first + lax.broadcasted_iota(jnp.int32, v.shape, 0)) < live
            sig[rows, at : at + wide] = jnp.where(keep, v, 0.0)
            at += wide
    sig_cp = pltpu.make_async_copy(sig, sig_out, load_sem.at[0])
    sig_cp.start()
    total = reduce_finish(1, red_zc, 7)
    energy = jnp.sum(total[0:4]) / jnp.sum(total[4:8])
    energy_row[...] = jnp.full((1, 1024), energy, F32)
    energy_cp = pltpu.make_async_copy(energy_row, energy_out, load_sem.at[1])
    energy_cp.start()

    drain(c_send, send_sem.at[0])
    for h in range(2):
        drain(othery[h], other_send.at[h])
        drain(otherz[h], other_send.at[2 + h])
        drain(rx[h], send_sem.at[2 + h])
        drain(rvx[h], send_sem.at[12 + h])
        drain(rux[h], send_sem.at[30 + h])
        for b in range(2):
            g = b * 2 + h
            drain(ry[b][h], send_sem.at[4 + g])
            drain(rz[b][h], send_sem.at[8 + g])
            drain(rxy[b][h], send_sem.at[14 + g])
            drain(rxz[b][h], send_sem.at[18 + g])
            drain(ruy[b][h], send_sem.at[22 + g])
            drain(ruz[b][h], send_sem.at[26 + g])
    drain(red_xy, red_send.at[0])
    drain(red_zc, red_send.at[1])
    for cp in state_cp + [sig_cp, energy_cp]:
        cp.wait()


def per_device(wavefunction, left_operator, right_operator, sector_size, term_shift):
    psi = wavefunction[0]
    hbm = pl.BlockSpec(memory_space=pl.ANY)
    out = jax.ShapeDtypeStruct((32, 1024), F32)
    row = jax.ShapeDtypeStruct((1, 1024), F32)
    sigma, state, energy, unit = pl.pallas_call(
        kernel,
        out_shape=(out, jax.ShapeDtypeStruct((32, 1024), BF), row, row),
        in_specs=[hbm] * 6,
        out_specs=(hbm, hbm, hbm, hbm),
        scratch_shapes=list(scratch().values()),
        compiler_params=pltpu.CompilerParams(
            collective_id=0, has_side_effects=True, vmem_limit_bytes=60 * 2**20
        ),
        name="sigma_step",
    )(
        term_shift,
        sector_size,
        psi,
        psi.reshape(4, 4, 2, 2, 16, 1024),
        left_operator[:, 0].reshape(4, 4, 4, 2, 2, 16, 1024),
        right_operator,
    )
    sigma = sigma * unit
    return sigma[None], (sigma - energy * state.astype(F32))[None]


def solution(mesh):
    finer = Mesh(mesh.devices.reshape(mesh.shape["sec"], 4, 4, 2), AXES)
    return jax.shard_map(
        per_device,
        mesh=finer,
        in_specs=(P("sec", None, None), P(OP, "sec", None, None), P(OP, None, None), P(), P()),
        out_specs=(P("sec", OP, None), P("sec", OP, None)),
        check_vma=False,
    )
```

```python
import jax
import jax.numpy as jnp
from jax import lax
from jax.experimental import pallas as pl
from jax.experimental.pallas import tpu as pltpu
from jax.sharding import Mesh
from jax.sharding import PartitionSpec as P

OP = ("op_0", "op_1", "op_2")
AXES = ("sec", "op_0", "op_1", "op_2")
MESH = pl.DeviceIdType.MESH
BF = jnp.bfloat16
F32 = jnp.float32
PAIRS = 8
ITEMS = 16
LAG = 3


def decode(p):
    return (p // 3, p % 3) if p < 6 else (p - 6, 3)


WX = (128, 0)
WY = ((256, 128), (256, 256))
WZ = ((128, 256), (256, 256))


def scratch():
    V = pltpu.VMEM
    DMA = pltpu.SemaphoreType.DMA
    out = {
        "psib": V((1024, 1024), BF),
        "image0": V((2, 256, 1024), BF),
        "image1": V((2, 256, 1024), BF),
        "rowsb": V((2, 2, 4, 4, 16, 512), BF),
        "c_send": V((ITEMS, 256, 512), BF),
        "c_recv": V((ITEMS, 256, 512), BF),
        "shift": pltpu.SMEM((128,), jnp.int32),
        "size": pltpu.SMEM((4,), jnp.int32),
        "sig": V((32, 1024), F32),
        "energy_row": V((1, 1024), F32),
        "unit_row": V((1, 1024), F32),
        "acc": V((16, 128), F32),
        "red": V((2, 8, 128), F32),
        "red_xy": V((15, 8, 128), F32),
        "red_zc": V((7, 8, 128), F32),
        "load_sem": DMA((13,)),
        "send_sem": DMA((32,)),
        "c_sem": DMA((ITEMS,)),
        "y_sem": DMA((ITEMS,)),
        "z_sem": DMA((ITEMS,)),
        "x_sem": DMA((2,)),
        "xy_sem": DMA((4,)),
        "xz_sem": DMA((4,)),
        "vx_sem": DMA((2,)),
        "ux_sem": DMA((2,)),
        "uy_sem": DMA((4,)),
        "uz_sem": DMA((4,)),
        "other_send": DMA((4,)),
        "other_recv": DMA((4,)),
        "red_send": DMA((2,)),
        "red_recv": DMA((2,)),
    }
    for h in range(2):
        out[f"left{h}"] = V((4, 2, 4, 4, 16, 1024), BF)
        out[f"right{h}"] = V((4, 1024, 512), BF)
        out[f"sx{h}"] = V((4, 4, 4, 16, WX[0]), BF)
        out[f"rx{h}"] = V((3, 4, 4, 16, WX[0]), BF)
        out[f"vx{h}"] = V((4, 4, 16, WX[0]), BF)
        out[f"fx{h}"] = V((4, 4, 16, WX[0]), F32)
        out[f"rvx{h}"] = V((3, 4, 16, WX[0]), BF)
        out[f"gx{h}"] = V((4, 16, WX[0]), F32)
        out[f"ux{h}"] = V((4, 16, WX[0]), BF)
        out[f"rux{h}"] = V((3, 16, WX[0]), BF)
        for name, widths in (("y", WY), ("z", WZ)):
            out[f"other{name}{h}"] = V((3, 4, 16, widths[1][h]), BF)
            for b in range(2):
                wide = widths[b][h]
                out[f"s{name}{b}{h}"] = V((4, 4, 4, 16, wide), BF)
                out[f"r{name}{b}{h}"] = V((4, 3, 4, 16, wide), BF)
                out[f"t{name}{b}{h}"] = V((3, 4, 16, wide), BF)
                out[f"rx{name}{b}{h}"] = V((3, 4, 16, wide), BF)
                out[f"to{name}{b}{h}"] = V((4, 16, wide), F32)
                out[f"u{name}{b}{h}"] = V((4, 16, wide), BF)
                out[f"ru{name}{b}{h}"] = V((3, 16, wide), BF)
    return out


def fold(v):
    wide = v.shape[-1]
    v = jnp.sum(v.reshape(-1, 8, wide), axis=0)
    return sum(v[:, i : i + 128] for i in range(0, wide, 128))


def kernel(shift_in, size_in, psi, psi_rows, left, right, sig_out, state_out, energy_out, unit_out, *held):
    ref = dict(zip(scratch(), held))

    def both(name):
        return ref[name + "0"], ref[name + "1"]

    def four(name):
        return both(name + "0"), both(name + "1")

    psib, image0, image1, rowsb, c_send, c_recv, acc, red, red_xy, red_zc = (
        ref[name]
        for name in (
            "psib", "image0", "image1", "rowsb", "c_send", "c_recv", "acc", "red", "red_xy", "red_zc"
        )
    )
    sig, energy_row, unit_row = ref["sig"], ref["energy_row"], ref["unit_row"]
    load_sem, send_sem, c_sem, y_sem, z_sem, x_sem = (
        ref[name] for name in ("load_sem", "send_sem", "c_sem", "y_sem", "z_sem", "x_sem")
    )
    othery, otherz = both("othery"), both("otherz")
    other_send, other_recv = ref["other_send"], ref["other_recv"]
    xy_sem, xz_sem, vx_sem, ux_sem, uy_sem, uz_sem, red_send, red_recv = (
        ref[name]
        for name in ("xy_sem", "xz_sem", "vx_sem", "ux_sem", "uy_sem", "uz_sem", "red_send", "red_recv")
    )
    sx, rx, vx, fx, rvx, gx, ux, rux = (both(name) for name in ("sx", "rx", "vx", "fx", "rvx", "gx", "ux", "rux"))
    sy, ry, ty, rxy, toy, uy, ruy = (four(name) for name in ("sy", "ry", "ty", "rxy", "toy", "uy", "ruy"))
    sz, rz, tz, rxz, toz, uz, ruz = (four(name) for name in ("sz", "rz", "tz", "rxz", "toz", "uz", "ruz"))
    x, z, y, c = (lax.axis_index(a) for a in AXES)
    group = z * 8 + y * 2 + c
    shift, size = ref["shift"], ref["size"]

    def ring(me, d):
        return lax.rem(me + d, 4)

    leftb = both("left")
    rightb = both("right")
    psi_cp = pltpu.make_async_copy(psi, psib, load_sem.at[0])
    halves = (1 - c, c)
    left_cp = [
        [
            pltpu.make_async_copy(left.at[:, :, :, halves[f], b], leftb[b].at[:, f], load_sem.at[1 + 2 * b + f])
            for f in range(2)
        ]
        for b in range(2)
    ]
    right_cp = [
        pltpu.make_async_copy(right.at[:, :, pl.ds(h * 512, 512)], rightb[h], load_sem.at[5 + h]) for h in range(2)
    ]
    rows_cp = [
        pltpu.make_async_copy(
            psi_rows.at[:, :, c, b, :, pl.ds(h * 512, 512)], rowsb.at[b, h], load_sem.at[7 + 2 * b + h]
        )
        for b in range(2)
        for h in range(2)
    ]
    scalar_cp = [
        pltpu.make_async_copy(size_in, size, load_sem.at[11]),
        pltpu.make_async_copy(shift_in, shift, load_sem.at[12]),
    ]
    psi_cp.start()
    for cp in scalar_cp + left_cp[0]:
        cp.start()

    barrier = pltpu.get_barrier_semaphore()
    for d in range(1, 4):
        for e in range(4):
            pl.semaphore_signal(
                barrier, inc=1, device_id={"sec": ring(x, d), "op_1": ring(y, e)}, device_id_type=MESH
            )
        pl.semaphore_signal(barrier, inc=1, device_id={"op_1": ring(y, d)}, device_id_type=MESH)
        pl.semaphore_signal(barrier, inc=1, device_id={"op_0": ring(z, d)}, device_id_type=MESH)
        pl.semaphore_signal(barrier, inc=1, device_id={"op_0": ring(z, d), "op_2": 1 - c}, device_id_type=MESH)
    pl.semaphore_signal(barrier, inc=1, device_id={"op_2": 1 - c}, device_id_type=MESH)

    for cp in scalar_cp:
        cp.wait()
    live = size[x]
    psi_cp.wait()
    right_cp[0].start()
    for i in range(4):
        at = slice(512 + i * 128, 640 + i * 128)
        pos = lax.broadcasted_iota(jnp.int32, (128, 1024), 0) + (512 + i * 128)
        psib[at, :] = jnp.where(pos < live, psib[at, :].astype(F32), 0.0).astype(BF)
    acc[...] = jnp.zeros_like(acc)

    def term_of(k):
        want = (k + 1) % 4
        t = 0
        for i in range(1, 4):
            t = jnp.where(shift[group * 4 + i] == want, i, t)
        return t

    def send(device, src, dst, sem_s, sem_r):
        return pltpu.make_async_remote_copy(
            src_ref=src, dst_ref=dst, send_sem=sem_s, recv_sem=sem_r, device_id=device, device_id_type=MESH
        )

    def to(axis, where, src, dst, sem_s, sem_r):
        return send({axis: where}, src, dst, sem_s, sem_r)

    def drain(ref, sem):
        pltpu.make_async_copy(ref, ref, sem).wait()

    def core_copy(n):
        return to("op_2", 1 - c, c_send.at[n], c_recv.at[n], send_sem.at[0], c_sem.at[n])

    def state(b, h):
        wx = WX[b]
        cut = wx + WY[b][h]
        return (
            lambda *at: rowsb[(b, h, *at, slice(None), slice(0, wx))].astype(F32),
            lambda *at: rowsb[(b, h, *at, slice(None), slice(wx, cut))].astype(F32),
            lambda *at: rowsb[(b, h, *at, slice(None), slice(cut, 512))].astype(F32),
        )

    every = slice(None)

    def left_step(p):
        b, k = decode(p)
        t = term_of(k)
        slot = p % 2
        a = leftb[b][t].reshape(512, 1024)
        for q in range(4):
            cols = slice(q * 256, (q + 1) * 256)
            o = jnp.dot(a, psib[:, cols], preferred_element_type=F32).astype(BF)
            image0[slot, :, cols] = o[:256]
            image1[slot, :, cols] = o[256:]

    def partner_half(p, halves):
        t = term_of(decode(p)[1])
        a = image0[p % 2]
        for h in halves:
            for q in range(2):
                cols = slice(q * 256, (q + 1) * 256)
                c_send[p * 2 + h, :, cols] = jnp.dot(
                    a, rightb[h][t, :, cols], preferred_element_type=F32
                ).astype(BF)
        for h in halves:
            core_copy(p * 2 + h).start()

    def own_half(p, halves):
        b, k = decode(p)
        t = term_of(k)
        for h in halves:
            core_copy(p * 2 + h).wait_recv()
        a = image1[p % 2]
        for h in halves:
            for q in range(2):
                cols = slice(q * 256, (q + 1) * 256)
                v = jnp.dot(a, rightb[h][t, :, cols], preferred_element_type=F32).astype(BF).astype(F32)
                v = (v + c_recv[p * 2 + h, :, cols].astype(F32)).astype(BF).reshape(4, 4, 16, 256)
                for j in range(2):
                    w = v[..., j * 128 : (j + 1) * 128]
                    at = q * 256 + j * 128
                    wx = WX[b]
                    cut = wx + WY[b][h]
                    if at < wx:
                        for i in range(4):
                            sx[h][k, i] = w[:, i]
                    elif at < cut:
                        for i in range(4):
                            sy[b][h][k, i, :, :, at - wx : at - wx + 128] = w[:, i]
                    else:
                        sz[b][h][k, :, :, :, at - cut : at - cut + 128] = w
        for h in halves:
            n = p * 2 + h
            for d in range(1, 4):
                yd = ring(y, d)
                zd = ring(z, d)
                to("op_1", yd, sy[b][h].at[k, yd], ry[b][h].at[k, d - 1], send_sem.at[4 + 2 * b + h], y_sem.at[n]).start()
                to("op_0", zd, sz[b][h].at[k, zd], rz[b][h].at[k, d - 1], send_sem.at[8 + 2 * b + h], z_sem.at[n]).start()

        if k < 3 and WX[b]:
            for h in halves:
                to("sec", ring(x, k + 1), sx[h].at[k], rx[h].at[k], send_sem.at[2 + h], x_sem.at[h]).start()

    def own_target(b, h):
        ox, oy, oz = state(b, h)
        part = jnp.zeros((8, 128), F32)
        if WX[b]:
            drain(rx[h], x_sem.at[h])
            for i in range(4):
                w = sx[h][3, i].astype(F32)
                for j in range(3):
                    w += rx[h][j, i].astype(F32)
                fx[h][i] = w
                vx[h][i] = w.astype(BF)
                part += fold(w * ox(every, i))
            for d in range(1, 4):
                yd = ring(y, d)
                to("op_1", yd, vx[h].at[yd], rvx[h].at[d - 1], send_sem.at[12 + h], vx_sem.at[h]).start()
        for i in range(4):
            part += fold(sy[b][h][3, i].astype(F32) * oy(every, i))
            part += fold(sz[b][h][3, i].astype(F32) * oz(i, every))
        acc[0:8] += part

    def second(p):
        b, k = decode(p)
        for h in range(2):
            n = p * 2 + h
            g = b * 2 + h
            drain(ry[b][h].at[k], y_sem.at[n])
            drain(rz[b][h].at[k], z_sem.at[n])
            vy = sy[b][h][k, y].astype(F32)
            vz = sz[b][h][k, z].astype(F32)
            for d in range(3):
                vy += ry[b][h][k, d].astype(F32)
                vz += rz[b][h][k, d].astype(F32)
            if k < 3:
                ty[b][h][k] = vy.astype(BF)
                tz[b][h][k] = vz.astype(BF)
                who = ring(x, k + 1)
                to("sec", who, ty[b][h].at[k], rxy[b][h].at[k], send_sem.at[14 + g], xy_sem.at[g]).start()
                to("sec", who, tz[b][h].at[k], rxz[b][h].at[k], send_sem.at[18 + g], xz_sem.at[g]).start()
            else:
                toy[b][h][...] = vy
                toz[b][h][...] = vz

    def cross_share(p):
        b, k = decode(p)
        there = size[ring(x, k + 1)]

        def row(outer, inner):
            return (
                lax.broadcasted_iota(jnp.int32, (4, 16, 128), 0) * outer
                + lax.broadcasted_iota(jnp.int32, (4, 16, 128), 1)
                + (inner + c * 32 + b * 16)
            )

        live_y = row(256, y * 64) < there
        live_z = row(64, z * 256) < there
        part = jnp.zeros((8, 128), F32)
        for h in range(2):
            for i in range(0, WY[1][h], 128):
                w = othery[h][k, :, :, i : i + 128].astype(F32)
                part += fold(ty[b][h][k, :, :, i : i + 128].astype(F32) * jnp.where(live_y, w, 0.0))
            for i in range(0, WZ[1][h], 128):
                w = otherz[h][k, :, :, i : i + 128].astype(F32)
                part += fold(tz[b][h][k, :, :, i : i + 128].astype(F32) * jnp.where(live_z, w, 0.0))
        acc[0:8] += part

    def mask_rows():
        for cp in rows_cp:
            cp.wait()
        for b in range(2):
            for h in range(2):
                for i in range(4):
                    pos = (
                        lax.broadcasted_iota(jnp.int32, (4, 16, 512), 0) * 64
                        + lax.broadcasted_iota(jnp.int32, (4, 16, 512), 1)
                        + (i * 256 + c * 32 + b * 16)
                    )
                    rowsb[b, h, i] = jnp.where(pos < live, rowsb[b, h, i].astype(F32), 0.0).astype(BF)
        norm = jnp.zeros((8, 128), F32)
        for b in range(2):
            for h in range(2):
                s = rowsb[b, h, z, y].astype(F32)
                norm += fold(s[:, :256] * s[:, :256]) + fold(s[:, 256:] * s[:, 256:])
        acc[8:16] = norm

    for cp in left_cp[0]:
        cp.wait()
    for cp in right_cp[1:] + left_cp[1] + rows_cp:
        cp.start()
    left_step(0)
    pl.semaphore_wait(barrier, 22)
    for k in range(3):
        who = ring(x, 3 - k)
        for h in range(2):
            cols_y = pl.ds(h * 512 + WX[1], WY[1][h])
            cols_z = pl.ds(h * 512 + WX[1] + WY[1][h], WZ[1][h])
            to("sec", who, psi_rows.at[:, y, c, 1, :, cols_y], othery[h].at[k], other_send.at[h], other_recv.at[h]).start()
            to("sec", who, psi_rows.at[z, :, c, 1, :, cols_z], otherz[h].at[k], other_send.at[2 + h], other_recv.at[2 + h]).start()
    right_cp[0].wait()
    partner_half(0, (0,))
    left_step(1)
    right_cp[1].wait()
    partner_half(0, (1,))
    mask_rows()

    for p in range(1, PAIRS):
        if p == 2:
            for cp in left_cp[1]:
                cp.wait()
        for halves in ((0, 1),) if p < PAIRS - 1 else ((0,), (1,)):
            partner_half(p, halves)
        own_half(p - 1, (0, 1))
        if p < PAIRS - 1:
            left_step(p + 1)
        else:
            for h in range(2):
                own_target(0, h)
        if p >= LAG:
            second(p - LAG)
    own_half(PAIRS - 1, (0,))
    own_half(PAIRS - 1, (1,))

    for h in range(2):
        _, oy, oz = state(0, h)
        drain(rxy[0][h], xy_sem.at[h])
        drain(rxz[0][h], xz_sem.at[h])
        ay = rxy[0][h][0].astype(F32) + rxy[0][h][1].astype(F32) + rxy[0][h][2].astype(F32)
        az = rxz[0][h][0].astype(F32) + rxz[0][h][1].astype(F32) + rxz[0][h][2].astype(F32)
        acc[0:8] += fold(ay * oy(every, y)) + fold(az * oz(z, every))
        drain(othery[h], other_recv.at[h])
        drain(otherz[h], other_recv.at[2 + h])
    cross_share(3)
    cross_share(4)
    for h in range(2):
        own_target(1, h)
    second(5)
    cross_share(5)
    groups = [(b, h) for b in range(2) for h in range(2)]

    def reduce_start(stage, dst, devices):
        for i, device in enumerate(devices):
            send(device, red.at[stage], dst.at[i], red_send.at[stage], red_recv.at[stage]).start()

    def reduce_finish(stage, dst, count):
        drain(dst, red_recv.at[stage])
        v = red[stage]
        for i in range(count):
            v += dst[i]
        return v

    unit_row[...] = jnp.ones_like(unit_row)
    state_cp = [
        pltpu.make_async_copy(
            rowsb.at[b, h, z, y],
            state_out.at[pl.ds(b * 16, 16), pl.ds(h * 512, 512)],
            load_sem.at[2 + b * 2 + h],
        )
        for b, h in groups
    ] + [pltpu.make_async_copy(unit_row, unit_out, load_sem.at[6])]
    for cp in state_cp:
        cp.start()

    red[0] = jnp.concatenate([acc[0:4] + acc[4:8], acc[8:12] + acc[12:16]], axis=0)
    plane = [{"sec": ring(x, i // 4), "op_1": ring(y, i % 4)} for i in range(1, 16)]
    reduce_start(0, red_xy, plane)

    for b in range(2):
        second(PAIRS - 2 + b)
        for h in range(2):
            g = b * 2 + h
            if b == 1:
                drain(rxy[b][h], xy_sem.at[g])
                drain(rxz[b][h], xz_sem.at[g])
            vy = toy[b][h][...]
            vz = toz[b][h][...]
            for d in range(3):
                vy += rxy[b][h][d].astype(F32)
                vz += rxz[b][h][d].astype(F32)
            toy[b][h][...] = vy
            toz[b][h][...] = vz
            uy[b][h][...] = vy.astype(BF)
            uz[b][h][...] = vz.astype(BF)
            for d in range(1, 4):
                zd = ring(z, d)
                yd = ring(y, d)
                to("op_0", zd, uy[b][h].at[zd], ruy[b][h].at[d - 1], send_sem.at[22 + g], uy_sem.at[g]).start()
                to("op_1", yd, uz[b][h].at[yd], ruz[b][h].at[d - 1], send_sem.at[26 + g], uz_sem.at[g]).start()
            if WX[b]:
                drain(rvx[h], vx_sem.at[h])
                v = fx[h][y]
                for d in range(3):
                    v += rvx[h][d].astype(F32)
                gx[h][...] = v
                ux[h][...] = v.astype(BF)
                for d in range(1, 4):
                    zd = ring(z, d)
                    to("op_0", zd, ux[h].at[zd], rux[h].at[d - 1], send_sem.at[30 + h], ux_sem.at[h]).start()
    red[1] = reduce_finish(0, red_xy, 15)
    stack = [{"op_0": ring(z, i // 2), "op_2": lax.rem(c + i % 2, 2)} for i in range(1, 8)]
    reduce_start(1, red_zc, stack)
    for b, h in groups:
        g = b * 2 + h
        drain(ruy[b][h], uy_sem.at[g])
        drain(ruz[b][h], uz_sem.at[g])
        vy = toy[b][h][z]
        vz = toz[b][h][y]
        for d in range(3):
            vy += ruy[b][h][d].astype(F32)
            vz += ruz[b][h][d].astype(F32)
        parts = [vy, vz]
        if WX[b]:
            drain(rux[h], ux_sem.at[h])
            v = gx[h][z]
            for d in range(3):
                v += rux[h][d].astype(F32)
            parts = [v] + parts
        first = z * 256 + y * 64 + c * 32 + b * 16
        rows = slice(b * 16, b * 16 + 16)
        at = h * 512
        for v in parts:
            wide = v.shape[-1]
            keep = (first + lax.broadcasted_iota(jnp.int32, v.shape, 0)) < live
            sig[rows, at : at + wide] = jnp.where(keep, v, 0.0)
            at += wide
    sig_cp = pltpu.make_async_copy(sig, sig_out, load_sem.at[0])
    sig_cp.start()
    total = reduce_finish(1, red_zc, 7)
    energy = jnp.sum(total[0:4]) / jnp.sum(total[4:8])
    energy_row[...] = jnp.full((1, 1024), energy, F32)
    energy_cp = pltpu.make_async_copy(energy_row, energy_out, load_sem.at[1])
    energy_cp.start()

    drain(c_send, send_sem.at[0])
    for h in range(2):
        drain(othery[h], other_send.at[h])
        drain(otherz[h], other_send.at[2 + h])
        drain(rx[h], send_sem.at[2 + h])
        drain(rvx[h], send_sem.at[12 + h])
        drain(rux[h], send_sem.at[30 + h])
        for b in range(2):
            g = b * 2 + h
            drain(ry[b][h], send_sem.at[4 + g])
            drain(rz[b][h], send_sem.at[8 + g])
            drain(rxy[b][h], send_sem.at[14 + g])
            drain(rxz[b][h], send_sem.at[18 + g])
            drain(ruy[b][h], send_sem.at[22 + g])
            drain(ruz[b][h], send_sem.at[26 + g])
    drain(red_xy, red_send.at[0])
    drain(red_zc, red_send.at[1])
    for cp in state_cp + [sig_cp, energy_cp]:
        cp.wait()


def per_device(wavefunction, left_operator, right_operator, sector_size, term_shift):
    psi = wavefunction[0]
    hbm = pl.BlockSpec(memory_space=pl.ANY)
    out = jax.ShapeDtypeStruct((32, 1024), F32)
    row = jax.ShapeDtypeStruct((1, 1024), F32)
    sigma, state, energy, unit = pl.pallas_call(
        kernel,
        out_shape=(out, jax.ShapeDtypeStruct((32, 1024), BF), row, row),
        in_specs=[hbm] * 6,
        out_specs=(hbm, hbm, hbm, hbm),
        scratch_shapes=list(scratch().values()),
        compiler_params=pltpu.CompilerParams(
            collective_id=0, has_side_effects=True, vmem_limit_bytes=60 * 2**20
        ),
        name="sigma_step",
    )(
        term_shift,
        sector_size,
        psi,
        psi.reshape(4, 4, 2, 2, 16, 1024),
        left_operator[:, 0].reshape(4, 4, 4, 2, 2, 16, 1024),
        right_operator,
    )
    sigma = sigma * unit
    return sigma[None], (sigma - energy * state.astype(F32))[None]


def solution(mesh):
    finer = Mesh(mesh.devices.reshape(mesh.shape["sec"], 4, 4, 2), AXES)
    return jax.shard_map(
        per_device,
        mesh=finer,
        in_specs=(P("sec", None, None), P(OP, "sec", None, None), P(OP, None, None), P(), P()),
        out_specs=(P("sec", OP, None), P("sec", OP, None)),
        check_vma=False,
    )
```
